256 devices in a mesh: user: 32 (over y, z_hi, core), item: 8 (over x, z_lo).
Axes of the slice: x: 4, y: 4, z: 8 (z_hi: 4, z_lo: 2; z = z_hi * 2 + z_lo), core: 2. Of those that a mesh axis runs over, the one named last changes fastest.
Arguments:
- observed: bfloat16 [256, 128, 128, 128], P(('user', 'item')), may hold values from -6 to 6
- user_block: int32 [256], P(('user', 'item')), may hold values from 0 to 3
- item_block: int32 [256], P(('user', 'item')), may hold values from 0 to 1
- stratum: int32 [256], P(('user', 'item')), may hold values from 0 to 7
- context_ids: int32 [256, 128], P(('user', 'item')), may hold values from 0 to 2047
- core_tensor: float32 [16384, 128], P(('user', 'item')), may hold values from -1 to 1
- user_factor: bfloat16 [16384, 128], P('user'), may hold values from -3 to 3
- item_factor: bfloat16 [2048, 128], P('item'), may hold values from -3 to 3
- context_factor: bfloat16 [2048, 128], P(('user', 'item')), may hold values from -3 to 3
Outputs:
- core_grad: float32 [16384, 128], P(('user', 'item'))
- user_grad: float32 [16384, 128], P(('user', 'item'))
- item_grad: float32 [2048, 128], P(('user', 'item'))
- context_grad: float32 [2048, 128], P(('user', 'item'))
The draws below stay inside these ranges and needn't reach their ends.
Inputs may be any that keep to these rules, and one draw needn't show every extreme that they name: `user_block`: user block within the tile's user index.
All inputs are finite; a program needn't handle non-finite values.
Results may differ from the reference program's by a relative error of at most 0.0031.
Values may be sent and summed in bfloat16 or wider, within the bound.
No kernel may reach another device: no remote copies, remote signals or barrier semaphores. Data moves between devices by JAX's collectives and lax.ppermute only.
A program may use at most 128 MiB of HBM per device.

```python
import math
import jax
import jax.numpy as jnp
from jax import lax

R1 = 128
R2 = 128
R3 = 128
BU = 128
BI = 128
KC = 128
TILES_DEV = 1
UB_DEV = 4
IB_DEV = 2
TILES = 256
NU = 16384
NI = 2048
NC = 2048
N_ITEM = 8


def set_ends(values, own_key, low, high):
    longest = values.shape.index(max(values.shape))
    spots = []
    for shift in (0, 1):
        where = [jax.random.randint(jax.random.fold_in(own_key, axis), (), 0, length) for axis, length in enumerate(values.shape)]
        where[longest] = (where[longest] + shift) % values.shape[longest]
        spots.append(tuple(where))
    return values.at[spots[0]].set(low).at[spots[1]].set(high)


def shard_levels(key, dims, shards, least, top_value):
    def one(dim, blocks):
        draws = jax.random.uniform(jax.random.fold_in(jax.random.fold_in(key, 6), dim), (blocks,), jnp.float32, least / len(shards), top_value / len(shards))
        return jnp.repeat(jnp.exp(draws), dims[dim] // blocks).reshape((-1,) + (1,) * (len(dims) - dim - 1))

    level = one(*shards[0])
    for cut in shards[1:]:
        level = level * one(*cut)
    return level


def normal_values(key, shape, scale, limit, shards=(), kind=jnp.bfloat16):
    gain = shard_levels(key, shape, shards, -0.22, 0.18) if shards else 1.0
    result = jax.random.normal(key, shape, jnp.float32) * scale * gain
    return jnp.minimum(jnp.maximum(result, -limit), limit).astype(kind)


def setup_inputs(seed: int = 0) -> dict:
    key_of = jax.random.split(jax.random.key(seed), 10)
    observed = normal_values(key_of[0], (TILES, BU, BI, KC), 1.0, 6.0, ((0, 256),))
    user_block = set_ends(jax.random.randint(key_of[1], (TILES,), 0, UB_DEV), jax.random.fold_in(key_of[1], 1), 0, UB_DEV - 1).astype(jnp.int32)
    item_block = set_ends(jax.random.randint(key_of[2], (TILES,), 0, IB_DEV), jax.random.fold_in(key_of[2], 1), 0, IB_DEV - 1).astype(jnp.int32)
    stratum = set_ends(jax.random.randint(key_of[3], (TILES,), 0, N_ITEM), jax.random.fold_in(key_of[3], 1), 0, N_ITEM - 1).astype(jnp.int32)
    context_ids = set_ends(jax.random.randint(key_of[4], (TILES, KC), 0, NC), jax.random.fold_in(key_of[4], 1), 0, NC - 1).astype(jnp.int32)
    core_tensor = normal_values(key_of[5], (R1 * R2, R3), 0.074, 1.0, ((0, 256),), jnp.float32)
    user_factor = normal_values(key_of[6], (NU, R1), 0.21, 3.0, ((0, 32),))
    item_factor = normal_values(key_of[7], (NI, R2), 0.21, 3.0, ((0, 8),))
    context_factor = normal_values(key_of[8], (NC, R3), 0.21, 3.0, ((0, 256),))
    return dict(observed=observed, user_block=user_block, item_block=item_block, stratum=stratum, context_ids=context_ids, core_tensor=core_tensor, user_factor=user_factor, item_factor=item_factor, context_factor=context_factor)


def tile_terms(core_half, user_rows, item_rows, ctx_rows, observed_tile):
    first_pass = jnp.dot(core_half, ctx_rows.T, preferred_element_type=jnp.float32).astype(jnp.bfloat16)
    first_cube = first_pass.reshape(R1, R2, KC)
    second = jnp.einsum('pqc,bq->pbc', first_cube.astype(jnp.float32), item_rows.astype(jnp.float32)).astype(jnp.bfloat16)
    second_flat = second.reshape(R1, BI * KC)
    predicted = jnp.dot(user_rows, second_flat, preferred_element_type=jnp.float32)
    residual = (predicted - observed_tile.reshape(BU, BI * KC).astype(jnp.float32)).astype(jnp.bfloat16)
    grad_user = jnp.dot(residual, second_flat.T, preferred_element_type=jnp.float32)
    back_flat = jnp.dot(user_rows.T, residual, preferred_element_type=jnp.float32).astype(jnp.bfloat16)
    back_cube = back_flat.reshape(R1, BI, KC)
    grad_item = jnp.einsum('pbc,pqc->bq', back_cube.astype(jnp.float32), first_cube.astype(jnp.float32))
    folded = jnp.einsum('pbc,bq->pqc', back_cube.astype(jnp.float32), item_rows.astype(jnp.float32)).astype(jnp.bfloat16)
    folded = folded.reshape(R1 * R2, KC)
    grad_ctx = jnp.dot(folded.T, core_half, preferred_element_type=jnp.float32)
    grad_core = jnp.dot(folded, ctx_rows, preferred_element_type=jnp.float32)
    return (grad_core, grad_user, grad_item, grad_ctx)

def reference(observed, user_block, item_block, stratum, context_ids, core_tensor, user_factor, item_factor, context_factor):
    core_half = core_tensor.astype(jnp.bfloat16)
    scale = 1.0 / math.sqrt(BU * BI * KC)
    tile_numbers = jnp.arange(TILES, dtype=jnp.int32)

    def step(carry, inputs):
        acc_core, acc_user, acc_item, acc_ctx = carry
        tile_data, ublock, iblock, item_shard, slice_ids, tile_number = inputs
        device = tile_number // TILES_DEV
        user_index = device // N_ITEM
        user_start = ((user_index * UB_DEV + ublock) * BU).astype(jnp.int32)
        item_start = ((item_shard * IB_DEV + iblock) * BI).astype(jnp.int32)
        user_rows = lax.dynamic_slice_in_dim(user_factor, user_start, BU, 0)
        item_rows = lax.dynamic_slice_in_dim(item_factor, item_start, BI, 0)
        ctx_rows = jnp.take(context_factor, slice_ids, axis=0)
        g_core, g_user, g_item, g_ctx = tile_terms(core_half, user_rows, item_rows, ctx_rows, tile_data)
        old_user = lax.dynamic_slice_in_dim(acc_user, user_start, BU, 0)
        acc_user = lax.dynamic_update_slice_in_dim(acc_user, old_user + g_user, user_start, 0)
        old_item = lax.dynamic_slice_in_dim(acc_item, item_start, BI, 0)
        acc_item = lax.dynamic_update_slice_in_dim(acc_item, old_item + g_item, item_start, 0)
        acc_ctx = acc_ctx.at[slice_ids].add(g_ctx)
        return ((acc_core + g_core, acc_user, acc_item, acc_ctx), None)
    init = (jnp.zeros((R1 * R2, R3), jnp.float32), jnp.zeros((NU, R1), jnp.float32), jnp.zeros((NI, R2), jnp.float32), jnp.zeros((NC, R3), jnp.float32))
    final, unused = lax.scan(step, init, (observed, user_block, item_block, stratum, context_ids, tile_numbers))
    acc_core, acc_user, acc_item, acc_ctx = final
    return (acc_core * scale, acc_user * scale, acc_item * scale, acc_ctx * scale)
```

```python
import math

import jax
import jax.numpy as jnp
from jax import lax
from jax.sharding import Mesh, PartitionSpec as P

BF = jnp.bfloat16
F32 = jnp.float32
ALL = ("y", "zh", "core", "x", "zl")
BIG = ("y", "x", "zl")
CORE_ROWS, CTX_ROWS, ITEM_ROWS = 64, 8, 8
ROWS = CORE_ROWS + CTX_ROWS + ITEM_ROWS


def dot_nt(left, right, precision=None):
    return lax.dot_general(
        left, right, (((1,), (1,)), ((), ())), precision=precision, preferred_element_type=F32
    )


def dot_tn(left, right):
    return lax.dot_general(left, right, (((0,), (0,)), ((), ())), preferred_element_type=F32)


def swap(value):
    return lax.ppermute(value, "core", [(0, 1), (1, 0)])


def gather_all(block):
    one = lax.all_to_all(
        jnp.broadcast_to(block[None], (4,) + block.shape), "zh", 0, 0, tiled=True
    )
    own = lax.all_to_all(
        jnp.broadcast_to(one[None], (32,) + one.shape), BIG, 0, 0, tiled=True
    ).reshape(4, 4, 2, 4, ROWS, 128)
    return own, swap(own)


def reduce_all(own, other):
    both = (own + swap(other).astype(F32)).astype(BF)
    parts = lax.all_to_all(both.reshape(32, 4, ROWS, 128), BIG, 0, 0, tiled=True)
    some = jnp.sum(parts.astype(F32), axis=0)
    last = lax.all_to_all(some, "zh", 0, 0, tiled=True)
    return jnp.sum(last, axis=0)


def tile_terms(core_half, user_rows, item_rows, ctx_rows, observed):
    rank_one = user_rows.shape[1]
    rank_two = item_rows.shape[1]
    block_user, block_item, slices = observed.shape
    first = dot_nt(core_half, ctx_rows).astype(BF)
    first_cube = first.reshape(rank_one, rank_two, slices)
    second = jnp.einsum(
        "pqc,bq->pbc", first_cube, item_rows, preferred_element_type=F32
    ).astype(BF)
    second_flat = second.reshape(rank_one, block_item * slices)
    predicted = jnp.dot(user_rows, second_flat, preferred_element_type=F32)
    residual = (predicted - observed.reshape(block_user, -1).astype(F32)).astype(BF)
    grad_user = dot_nt(residual, second_flat)
    back = dot_tn(user_rows, residual).astype(BF).reshape(rank_one, block_item, slices)
    grad_item = jnp.einsum("pbc,pqc->bq", back, first_cube, preferred_element_type=F32)
    folded = jnp.einsum("pbc,bq->pqc", back, item_rows, preferred_element_type=F32)
    folded = folded.astype(BF).reshape(rank_one * rank_two, slices)
    grad_ctx = dot_tn(folded, core_half)
    grad_core = jnp.dot(folded, ctx_rows, preferred_element_type=F32)
    return grad_core, grad_user, grad_item, grad_ctx


def local(
    observed,
    user_block,
    item_block,
    stratum,
    context_ids,
    core_tensor,
    user_factor,
    item_factor,
    context_factor,
):
    y, zh, core, x, zl = (lax.axis_index(name) for name in ALL)
    scale = 1.0 / math.sqrt(128 * 128 * 128)
    ub, ib, st, ids = user_block[0], item_block[0], stratum[0], context_ids[0]
    mine = (y * 4 + zh) * 2 + core
    item_own = lax.dynamic_slice_in_dim(item_factor, mine * ITEM_ROWS, ITEM_ROWS, 0)
    block = jnp.concatenate([core_tensor.astype(BF), context_factor, item_own], axis=0)
    own, other = gather_all(block)
    both = jnp.stack([own, other])

    core_half = both[..., :CORE_ROWS, :].transpose(0, 1, 4, 2, 3, 5, 6).reshape(16384, 128)
    def spot_of(row):
        j, d = row & 7, row >> 3
        d_zl, d_x, d_c, d_zh, d_y = d & 1, (d >> 1) & 3, (d >> 3) & 1, (d >> 4) & 3, d >> 6
        place = ((((d_c ^ core) * 4 + d_y) * 4 + d_x) * 2 + d_zl) * 4 + d_zh
        return place * 8 + j

    spot = spot_of(ids)
    item_spot = spot_of((st * 2 + ib) * 128 + jnp.arange(128, dtype=jnp.int32))
    ctx_table = both[..., CORE_ROWS : CORE_ROWS + CTX_ROWS, :].reshape(2048, 128)
    ctx_rows = jnp.take(ctx_table, spot, axis=0)
    item_table = both[..., CORE_ROWS + CTX_ROWS :, :]
    picked = lax.dynamic_slice(
        item_table, (0, ib * 2, st // 2, st % 2, 0, 0, 0), (2, 2, 1, 1, 4, 8, 128)
    ).reshape(2, 2, 4, 8, 128)
    picked = jnp.where(core == 0, picked, picked[::-1])
    item_rows = picked.transpose(1, 2, 0, 3, 4).reshape(128, 128)
    user_rows = lax.dynamic_slice_in_dim(user_factor, ub * 128, 128, 0)
    col = jnp.arange(128, dtype=jnp.int32)
    true_p = ((col % 64) // 4) * 8 + ((col // 64) ^ core) * 4 + col % 4
    mix = (col[:, None] == true_p[None, :])
    user_perm = jnp.dot(user_rows, mix.astype(BF), preferred_element_type=F32).astype(BF)

    g_core, g_user, g_item, g_ctx = tile_terms(
        core_half, user_perm, item_rows, ctx_rows, observed[0]
    )

    send_core = g_core.reshape(2, 4, 4, 4, 2, CORE_ROWS, 128).transpose(0, 1, 3, 4, 2, 5, 6)
    places = jnp.arange(2048, dtype=jnp.int32)
    picker = (places[:, None] == spot[None, :]).astype(F32)
    send_ctx = jnp.dot(
        picker, g_ctx, precision=lax.Precision.HIGHEST, preferred_element_type=F32
    ).reshape(2, 4, 4, 2, 4, CTX_ROWS, 128)
    send_item = jnp.dot(
        (places[:, None] == item_spot[None, :]).astype(F32),
        g_item, precision=lax.Precision.HIGHEST, preferred_element_type=F32,
    ).reshape(2, 4, 4, 2, 4, ITEM_ROWS, 128)
    send = jnp.concatenate([send_core, send_ctx, send_item], axis=5)
    total = reduce_all(send[0], send[1].astype(BF)) * scale

    g_user = dot_nt(g_user, mix.astype(F32), precision=lax.Precision.HIGHEST)
    x_here = (jnp.arange(4) == ub)[:, None, None, None]
    send_user = jnp.where(x_here, g_user.reshape(1, 2, 64, 128), 0.0).astype(BF)
    got_user = lax.all_to_all(send_user.reshape(8, 64, 128), ("x", "zl"), 0, 0, tiled=True)
    user_grad = jnp.sum(got_user.astype(F32), axis=0) * scale
    return (
        total[:CORE_ROWS],
        user_grad,
        total[CORE_ROWS + CTX_ROWS :],
        total[CORE_ROWS : CORE_ROWS + CTX_ROWS],
    )


def solution(mesh):
    fine = Mesh(mesh.devices.reshape(4, 4, 2, 4, 2), ALL)
    user, item = ("y", "zh", "core"), ("x", "zl")
    return jax.shard_map(
        local,
        mesh=fine,
        in_specs=(
            P(ALL, None, None, None),
            P(ALL),
            P(ALL),
            P(ALL),
            P(ALL, None),
            P(ALL, None),
            P(user, None),
            P(item, None),
            P(ALL, None),
        ),
        out_specs=(P(ALL, None),) * 4,
        check_vma=False,
    )
```

```python
import math

import jax
import jax.numpy as jnp
from jax import lax
from jax.sharding import Mesh, PartitionSpec as P

BF = jnp.bfloat16
F32 = jnp.float32
ALL = ("y", "zh", "core", "x", "zl")
BIG = ("y", "x", "zl")
CORE_ROWS, CTX_ROWS, ITEM_ROWS = 64, 8, 8
ROWS = CORE_ROWS + CTX_ROWS + ITEM_ROWS


def dot_nt(left, right, precision=None):
    return lax.dot_general(
        left, right, (((1,), (1,)), ((), ())), precision=precision, preferred_element_type=F32
    )


def dot_tn(left, right):
    return lax.dot_general(left, right, (((0,), (0,)), ((), ())), preferred_element_type=F32)


def swap(value):
    return lax.ppermute(value, "core", [(0, 1), (1, 0)])


def gather_all(block, beside):
    one = lax.all_to_all(
        jnp.broadcast_to(block[None], (4,) + block.shape), "zh", 0, 0, tiled=True
    ).reshape(4 * ROWS, 128)
    one, beside = lax.optimization_barrier((one, beside))
    beside = beside.reshape(128, 16384)
    own = lax.all_to_all(jnp.broadcast_to(one[None], (32,) + one.shape), BIG, 0, 0, tiled=True)
    own, beside = lax.optimization_barrier((own, beside))
    own = own.reshape(4, 4, 2, 4, ROWS, 128)
    return own, swap(own), beside


def local(
    observed,
    user_block,
    item_block,
    stratum,
    context_ids,
    core_tensor,
    user_factor,
    item_factor,
    context_factor,
):
    y, zh, core, x, zl = (lax.axis_index(name) for name in ALL)
    scale = 1.0 / math.sqrt(128 * 128 * 128)
    ub, ib, st, ids = user_block[0], item_block[0], stratum[0], context_ids[0]
    mine = (y * 4 + zh) * 2 + core
    item_own = lax.dynamic_slice_in_dim(item_factor, mine * ITEM_ROWS, ITEM_ROWS, 0)
    block = jnp.concatenate([core_tensor.astype(BF), context_factor, item_own], axis=0)
    own, other, seen = gather_all(block, observed[0])
    both = jnp.stack([own, other])

    core_half = both[..., :CORE_ROWS, :].transpose(0, 1, 2, 4, 3, 5, 6).reshape(16384, 128)
    def spot_of(row):
        j, d = row & 7, row >> 3
        d_zl, d_x, d_c, d_zh, d_y = d & 1, (d >> 1) & 3, (d >> 3) & 1, (d >> 4) & 3, d >> 6
        place = ((((d_c ^ core) * 4 + d_y) * 4 + d_x) * 2 + d_zl) * 4 + d_zh
        return place * 8 + j

    spot = spot_of(ids)
    item_spot = spot_of((st * 2 + ib) * 128 + jnp.arange(128, dtype=jnp.int32))
    ctx_table = both[..., CORE_ROWS : CORE_ROWS + CTX_ROWS, :].reshape(2048, 128)
    ctx_rows = jnp.take(ctx_table, spot, axis=0)
    item_table = both[..., CORE_ROWS + CTX_ROWS :, :]
    picked = lax.dynamic_slice(
        item_table, (0, ib * 2, st // 2, st % 2, 0, 0, 0), (2, 2, 1, 1, 4, 8, 128)
    ).reshape(2, 2, 4, 8, 128)
    picked = jnp.where(core == 0, picked, picked[::-1])
    item_rows = picked.transpose(1, 2, 0, 3, 4).reshape(128, 128)
    user_rows = lax.dynamic_slice_in_dim(user_factor, ub * 128, 128, 0)
    col = jnp.arange(128, dtype=jnp.int32)
    true_p = ((col >> 4) & 3) * 32 + (col & 3) * 8 + ((col >> 6) ^ core) * 4 + ((col >> 2) & 3)
    mix = (col[:, None] == true_p[None, :])
    user_perm = jnp.dot(user_rows, mix.astype(BF), preferred_element_type=F32).astype(BF)

    first = dot_nt(core_half, ctx_rows).astype(BF).reshape(128, 128, 128)
    second = jnp.einsum("pqc,bq->pbc", first, item_rows, preferred_element_type=F32)
    second = second.astype(BF).reshape(128, 16384)
    predicted = jnp.dot(user_perm, second, preferred_element_type=F32)
    residual = (predicted - seen.astype(F32)).astype(BF)
    g_user = dot_nt(residual, second)
    back = dot_tn(user_perm, residual).astype(BF).reshape(128, 128, 128)
    folded = jnp.einsum("pbc,bq->pqc", back, item_rows, preferred_element_type=F32)
    folded = folded.astype(BF).reshape(16384, 128)
    g_other = jnp.dot(folded[8192:], ctx_rows, preferred_element_type=F32).astype(BF)
    got_core = swap(g_other)
    g_item = jnp.einsum("pbc,pqc->bq", back, first, preferred_element_type=F32)
    g_ctx = dot_tn(folded, core_half)

    places = jnp.arange(2048, dtype=jnp.int32)
    send_ctx = jnp.dot(
        (places[:, None] == spot[None, :]).astype(F32),
        g_ctx, precision=lax.Precision.HIGHEST, preferred_element_type=F32,
    )
    send_item = jnp.dot(
        (places[:, None] == item_spot[None, :]).astype(F32),
        g_item, precision=lax.Precision.HIGHEST, preferred_element_type=F32,
    )
    send = jnp.stack([send_ctx, send_item]).reshape(2, 2, 1024, 128)
    small = (send[:, 0] + swap(send[:, 1].astype(BF)).astype(F32)).astype(BF)
    small = small.reshape(2, 32, 4, 8, 128).transpose(1, 2, 0, 3, 4).reshape(32, 4, 16, 128)
    g_own = jnp.dot(folded[:8192], ctx_rows, preferred_element_type=F32)
    core_sum = (g_own + got_core.astype(F32)).astype(BF)
    core_sum = core_sum.reshape(4, 4, 4, 2, CORE_ROWS, 128).transpose(0, 1, 3, 2, 4, 5)
    both = jnp.concatenate([core_sum.reshape(32, 4, CORE_ROWS, 128), small], axis=2)
    parts = lax.all_to_all(both.reshape(32, 4 * ROWS, 128), BIG, 0, 0, tiled=True)

    g_user = dot_nt(g_user, mix.astype(F32), precision=lax.Precision.HIGHEST)
    x_here = (jnp.arange(4) == ub)[:, None, None, None]
    send_user = jnp.where(x_here, g_user.reshape(1, 2, 64, 128), 0.0).astype(BF)
    got_user = lax.all_to_all(send_user.reshape(8, 64, 128), ("x", "zl"), 0, 0, tiled=True)
    user_grad = jnp.sum(got_user.astype(F32), axis=0) * scale

    some = jnp.sum(parts.astype(F32), axis=0).reshape(4, ROWS, 128)
    last = lax.all_to_all(some, "zh", 0, 0, tiled=True)
    total = jnp.sum(last, axis=0) * scale
    return (
        total[:CORE_ROWS],
        user_grad,
        total[CORE_ROWS + CTX_ROWS :],
        total[CORE_ROWS : CORE_ROWS + CTX_ROWS],
    )


def solution(mesh):
    fine = Mesh(mesh.devices.reshape(4, 4, 2, 4, 2), ALL)
    user, item = ("y", "zh", "core"), ("x", "zl")
    return jax.shard_map(
        local,
        mesh=fine,
        in_specs=(
            P(ALL, None, None, None),
            P(ALL),
            P(ALL),
            P(ALL),
            P(ALL, None),
            P(ALL, None),
            P(user, None),
            P(item, None),
            P(ALL, None),
        ),
        out_specs=(P(ALL, None),) * 4,
        check_vma=False,
    )
```

```python
import math

import jax
import jax.numpy as jnp
from jax import lax
from jax.sharding import Mesh, PartitionSpec as P

BF = jnp.bfloat16
F32 = jnp.float32
ALL = ("y", "zh", "core", "x", "zl")
REST = ("y", "zh", "zl")
CORE_ROWS, CTX_ROWS, ITEM_ROWS = 64, 8, 8
ROWS = CORE_ROWS + CTX_ROWS + ITEM_ROWS


def dot_nt(left, right, precision=None):
    return lax.dot_general(
        left, right, (((1,), (1,)), ((), ())), precision=precision, preferred_element_type=F32
    )


def dot_tn(left, right):
    return lax.dot_general(left, right, (((0,), (0,)), ((), ())), preferred_element_type=F32)


def swap(value):
    return lax.ppermute(value, "core", [(0, 1), (1, 0)])


def shift(value, by):
    return lax.ppermute(value, "x", [(i, (i + by) % 4) for i in range(4)])


def gather_all(block, beside):
    copies = jnp.broadcast_to(block[None], (32,) + block.shape)
    own = lax.all_to_all(copies, REST, 0, 0, tiled=True)
    own, beside = lax.optimization_barrier((own, beside))
    beside = beside.reshape(128, 16384)
    before, after = shift(own, 1), shift(own, -1)
    own_other = swap(own)
    before, after, own_other, beside = lax.optimization_barrier(
        (before, after, own_other, beside)
    )
    far = [shift(before[:16], 1), shift(after[16:], -1)]
    mine = [own, before, after] + far
    other = [own_other] + [swap(piece) for piece in mine[1:]]
    return mine + other, beside


def reduce_all(blocks):
    half = 16 * ROWS
    up, down = shift(blocks[3, :half], 1), shift(blocks[3, half:], -1)
    to_up = (blocks[2, :half].astype(F32) + up.astype(F32)).astype(BF)
    to_down = (blocks[1, half:].astype(F32) + down.astype(F32)).astype(BF)
    from_low = shift(jnp.concatenate([to_up, blocks[2, half:]]), 1)
    from_high = shift(jnp.concatenate([blocks[1, :half], to_down]), -1)
    total = blocks[0].astype(F32) + from_low.astype(F32) + from_high.astype(F32)
    last = lax.all_to_all(
        total.astype(BF).reshape(32, ROWS, 128), REST, 0, 0, tiled=True
    )
    return jnp.sum(last.astype(F32), axis=0)


def local(
    observed,
    user_block,
    item_block,
    stratum,
    context_ids,
    core_tensor,
    user_factor,
    item_factor,
    context_factor,
):
    y, zh, core, x, zl = (lax.axis_index(name) for name in ALL)
    scale = 1.0 / math.sqrt(128 * 128 * 128)
    ub, ib, st, ids = user_block[0], item_block[0], stratum[0], context_ids[0]
    mine = (y * 4 + zh) * 2 + core
    item_own = lax.dynamic_slice_in_dim(item_factor, mine * ITEM_ROWS, ITEM_ROWS, 0)
    block = jnp.concatenate([core_tensor.astype(BF), context_factor, item_own], axis=0)
    pieces, seen = gather_all(block, observed[0])

    def cut(low, high):
        return jnp.concatenate([piece[:, low:high] for piece in pieces])

    core_half = cut(0, CORE_ROWS).reshape(16384, 128)

    def slot_of(at_x):
        apart = (at_x - x) & 3
        return jnp.where(apart == 0, 0, jnp.where(apart == 3, 1, apart + 1))

    def spot_of(row):
        j, d = row & 7, row >> 3
        d_zl, d_x, d_c, d_zh, d_y = d & 1, (d >> 1) & 3, (d >> 3) & 1, (d >> 4) & 3, d >> 6
        place = ((((d_c ^ core) * 4 + slot_of(d_x)) * 4 + d_y) * 4 + d_zh) * 2 + d_zl
        return place * 8 + j

    spot = spot_of(ids)
    item_spot = spot_of((st * 2 + ib) * 128 + jnp.arange(128, dtype=jnp.int32))
    ctx_table = cut(CORE_ROWS, CORE_ROWS + CTX_ROWS).reshape(2048, 128)
    ctx_rows = jnp.take(ctx_table, spot, axis=0)
    item_table = cut(CORE_ROWS + CTX_ROWS, ROWS).reshape(2, 4, 4, 4, 2, ITEM_ROWS, 128)
    picked = lax.dynamic_slice(
        item_table, (0, slot_of(st // 2), ib * 2, 0, st % 2, 0, 0), (2, 1, 2, 4, 1, 8, 128)
    ).reshape(2, 2, 4, 8, 128)
    picked = jnp.where(core == 0, picked, picked[::-1])
    item_rows = picked.transpose(1, 2, 0, 3, 4).reshape(128, 128)
    user_rows = lax.dynamic_slice_in_dim(user_factor, ub * 128, 128, 0)
    col = jnp.arange(128, dtype=jnp.int32)
    slot = (col >> 4) & 3
    apart = jnp.where(slot == 0, 0, jnp.where(slot == 1, 3, slot - 1))
    true_p = (col & 15) * 8 + ((col >> 6) ^ core) * 4 + ((x + apart) & 3)
    mix = (col[:, None] == true_p[None, :])
    user_perm = jnp.dot(user_rows, mix.astype(BF), preferred_element_type=F32).astype(BF)

    first = dot_nt(core_half, ctx_rows).astype(BF).reshape(128, 128, 128)
    second = jnp.einsum("pqc,bq->pbc", first, item_rows, preferred_element_type=F32)
    second = second.astype(BF).reshape(128, 16384)
    predicted = jnp.dot(user_perm, second, preferred_element_type=F32)
    residual = (predicted - seen.astype(F32)).astype(BF)
    g_user = dot_nt(residual, second)
    back = dot_tn(user_perm, residual).astype(BF).reshape(128, 128, 128)
    folded = jnp.einsum("pbc,bq->pqc", back, item_rows, preferred_element_type=F32)
    folded = folded.astype(BF).reshape(16384, 128)
    g_other = jnp.dot(folded[8192:], ctx_rows, preferred_element_type=F32).astype(BF)
    got_core = swap(g_other)
    g_item = jnp.einsum("pbc,pqc->bq", back, first, preferred_element_type=F32)
    g_ctx = dot_tn(folded, core_half)

    places = jnp.arange(2048, dtype=jnp.int32)
    send_ctx = jnp.dot(
        (places[:, None] == spot[None, :]).astype(F32),
        g_ctx, precision=lax.Precision.HIGHEST, preferred_element_type=F32,
    )
    send_item = jnp.dot(
        (places[:, None] == item_spot[None, :]).astype(F32),
        g_item, precision=lax.Precision.HIGHEST, preferred_element_type=F32,
    )
    send = jnp.stack([send_ctx, send_item]).reshape(2, 2, 1024, 128)
    small = (send[:, 0] + swap(send[:, 1].astype(BF)).astype(F32)).astype(BF)
    small = small.reshape(2, 128, 8, 128).transpose(1, 0, 2, 3).reshape(128, 16, 128)
    g_own = jnp.dot(folded[:8192], ctx_rows, preferred_element_type=F32)
    core_sum = (g_own + got_core.astype(F32)).astype(BF).reshape(128, CORE_ROWS, 128)
    blocks = jnp.concatenate([core_sum, small], axis=1).reshape(4, 32 * ROWS, 128)
    total = reduce_all(blocks) * scale

    g_user = dot_nt(g_user, mix.astype(F32), precision=lax.Precision.HIGHEST)
    x_here = (jnp.arange(4) == ub)[:, None, None, None]
    send_user = jnp.where(x_here, g_user.reshape(1, 2, 64, 128), 0.0)
    keep = lax.dynamic_index_in_dim(send_user, zl, 1, keepdims=False)
    give = lax.dynamic_index_in_dim(send_user, 1 - zl, 1, keepdims=False)
    got = lax.ppermute(give.astype(BF), "zl", [(0, 1), (1, 0)])
    half_user = keep + got.astype(F32)
    user_sum = lax.dynamic_index_in_dim(half_user, x, 0, keepdims=False)
    for by in (1, 2, 3):
        give = lax.dynamic_index_in_dim(half_user, (x + by) & 3, 0, keepdims=False)
        user_sum = user_sum + shift(give.astype(BF), by).astype(F32)
    return (
        total[:CORE_ROWS],
        user_sum * scale,
        total[CORE_ROWS + CTX_ROWS :],
        total[CORE_ROWS : CORE_ROWS + CTX_ROWS],
    )


def solution(mesh):
    fine = Mesh(mesh.devices.reshape(4, 4, 2, 4, 2), ALL)
    user, item = ("y", "zh", "core"), ("x", "zl")

    return jax.shard_map(
        local,
        mesh=fine,
        in_specs=(
            P(ALL, None, None, None),
            P(ALL),
            P(ALL),
            P(ALL),
            P(ALL, None),
            P(ALL, None),
            P(user, None),
            P(item, None),
            P(ALL, None),
        ),
        out_specs=(P(ALL, None),) * 4,
        check_vma=False,
    )
```
